512 devices in a mesh: rows: 128 (over z, y, core), cols: 4 (over x).
Axes of the slice: x: 4, y: 4, z: 16, core: 2. Of those that a mesh axis runs over, the one named last changes fastest.
Arguments:
- embeddings: bfloat16 [131072, 1024], P('rows'), may hold values from -6 to 6
- knn_mean: bfloat16 [131072], P('rows'), may hold values from 0.29882812 to 0.8984375
- pair_rows: int32 [128, 4, 24], P('rows', 'cols'), may hold values from 0 to 511, as said below
- pair_cols: int32 [128, 4, 24], P('rows', 'cols'), may hold values from 0 to 511, as said below
- pair_count: int32 [128, 4], P('rows', 'cols'), may hold values from 2 to 24, as said below
- start_block: float32 [64, 131072], P(None, 'rows')
Outputs:
- block_vector: float32 [64, 131072], P(None, 'rows')
The draws below stay inside these ranges and needn't reach their ends.
Inputs may be any that keep to these rules, and one draw needn't show every extreme that they name: `pair_count`: on every index of rows one device of cols has exactly 24 live slots. `pair_rows`: A live entry of device (i, j) is one of the row blocks i * 4 to (i + 1) * 4 - 1; the live pairs of one index of rows are all different, and each of its row blocks is paired with itself. Slots at pair_count and beyond are unused and repeat the device's first pair. `pair_cols`: the column block of a live pair of device (i, j) is a row block of rows index i - 1, i or i + 1.
All inputs are finite; a program needn't handle non-finite values.
Results may differ from the reference program's by a relative error of at most 0.0065.
Values may be sent and summed in bfloat16 or wider, within the bound.
A program may use at most 64 MiB of HBM per device.

```python
import math
import jax
import jax.numpy as jnp
from jax import lax

E = 1024
K = 64
BLOCK = 256
BLK_DEV = 4
ITERS = 2
PAIRS_DEV = 24
SENTENCES = 131072
N_ROWS = 128
N_COLS = 4


def pair_tables(key):
    base = jax.random.fold_in(key, 4242)
    key_count, key_full, key_order = jax.random.split(base, 3)
    span = 3 * BLK_DEV
    number = BLK_DEV * span
    index = jnp.arange(number, dtype=jnp.int32)
    row_local = index // span
    window = index % span
    groups = jnp.arange(N_ROWS, dtype=jnp.int32)[:, None]
    column = (groups - 1) * BLK_DEV + window[None, :]
    valid = (column >= 0) & (column < N_ROWS * BLK_DEV)
    valid_count = jnp.sum(valid.astype(jnp.int32), axis=1)
    room = (valid_count - PAIRS_DEV) // (N_COLS - 1)
    counts = jax.random.randint(key_count, (N_ROWS, N_COLS), BLK_DEV, 3 * BLK_DEV, dtype=jnp.int32)
    counts = jnp.maximum(jnp.minimum(counts, room[:, None]), 2)
    full = jax.random.randint(key_full, (N_ROWS,), 0, N_COLS, dtype=jnp.int32)
    lanes = jnp.arange(N_COLS, dtype=jnp.int32)
    counts = jnp.where(lanes[None, :] == full[:, None], jnp.int32(PAIRS_DEV), counts)
    diagonal = window == row_local + BLK_DEV
    noise = jax.random.randint(key_order, (N_ROWS, number), 0, 65536, dtype=jnp.int32)
    score = noise * number + index[None, :] + number
    score = jnp.where(diagonal[None, :], jnp.broadcast_to(index[None, :], score.shape), score)
    score = jnp.where(valid, score, score + 268435456)
    order = jnp.argsort(score, axis=1).astype(jnp.int32)
    offsets = jnp.cumsum(counts, axis=1) - counts
    slots = jnp.arange(PAIRS_DEV, dtype=jnp.int32)
    position = offsets[:, :, None] + slots[None, None, :]
    position = jnp.where(slots[None, None, :] < counts[:, :, None], position, jnp.broadcast_to(offsets[:, :, None], position.shape))
    chosen = jnp.take_along_axis(jnp.broadcast_to(order[:, None, :], (N_ROWS, N_COLS, number)), position, axis=2)
    rows_out = groups[:, :, None] * BLK_DEV + chosen // span
    cols_out = (groups[:, :, None] - 1) * BLK_DEV + chosen % span
    return (rows_out.astype(jnp.int32), cols_out.astype(jnp.int32), counts.astype(jnp.int32))


def draw_pair_rows(key, part):
    return pair_tables(key)[0]


def draw_pair_cols(key, part):
    return pair_tables(key)[1]


def draw_pair_count(key, part):
    return pair_tables(key)[2]


def draw_start_block(key, part):
    place = jnp.arange(SENTENCES, dtype=jnp.float32) / SENTENCES
    rising = jnp.exp(math.log(3.0) * place)[None, :]
    result = jax.random.normal(key, (K, SENTENCES), jnp.float32) * rising
    return result.astype(jnp.float32)


def steps_of(stream_key, dims, cuts, least, top_value):
    factor_of, own = 1.0, jax.random.fold_in(stream_key, 6)
    for dim, blocks in cuts:
        draws = jnp.exp(jax.random.uniform(jax.random.fold_in(own, dim), (blocks,), jnp.float32, least / len(cuts), top_value / len(cuts)))
        factor_of = factor_of * jnp.repeat(draws, dims[dim] // blocks).reshape([-1 if axis == dim else 1 for axis in range(len(dims))])
    return factor_of


def gaussian(stream_key, shape, spread, bound, cuts=(), kind=jnp.bfloat16):
    drawn = spread * jax.random.normal(stream_key, shape, jnp.float32)
    if cuts:
        drawn = drawn * steps_of(stream_key, shape, cuts, -0.22, 0.18)
    return jnp.clip(drawn, -bound, bound).astype(kind)


def setup_inputs(seed: int = 0) -> dict:
    splits = jax.random.split(jax.random.key(seed), 7)
    return {
        "embeddings": gaussian(splits[0], (SENTENCES, E), 1.0, 6.0, ((0, 128),)),
        "knn_mean": jnp.clip(jnp.exp(math.log(0.8984375) - 1.1007886 * jax.random.uniform(splits[1], (SENTENCES,), jnp.float32) ** steps_of(splits[1], (SENTENCES,), ((0, 128),), -0.2, 0.2)), 0.29882812, 0.8984375).astype(jnp.bfloat16),
        "pair_rows": draw_pair_rows(jax.random.fold_in(splits[6], 71), 0),
        "pair_cols": draw_pair_cols(jax.random.fold_in(splits[6], 71), 0),
        "pair_count": draw_pair_count(jax.random.fold_in(splits[6], 71), 0),
        "start_block": draw_start_block(jax.random.fold_in(splits[6], 71), 0),
    }


sharpness = 10.0
epsilon = 1e-06

def unit_rows(embeddings):
    values = embeddings.astype(jnp.float32)
    scale = lax.rsqrt(lax.optimization_barrier(jnp.mean(values * values, axis=1, keepdims=True)) + epsilon)
    return (values * scale / math.sqrt(values.shape[1])).astype(jnp.bfloat16)

def make_affinity(row_unit, col_unit, row_mean, col_mean, row_block, col_block):
    size = row_unit.shape[0]
    scores = lax.dot_general(row_unit.astype(jnp.float32), col_unit.astype(jnp.float32), (((1,), (1,)), ((), ())), preferred_element_type=jnp.float32)
    denom = 0.5 * (row_mean.astype(jnp.float32)[:, None] + col_mean.astype(jnp.float32)[None, :])
    weights = jnp.exp(sharpness * scores / denom)
    offsets = jnp.arange(size, dtype=jnp.int32)
    same = (row_block * size + offsets)[:, None] == (col_block * size + offsets)[None, :]
    return jnp.where(same, jnp.zeros_like(weights), weights).astype(jnp.bfloat16)

def add_block(accum, piece, block_index):
    size = piece.shape[1]
    current = lax.dynamic_slice_in_dim(accum, block_index * size, size, 1)
    return lax.dynamic_update_slice_in_dim(accum, current + piece, block_index * size, 1)

def reference(embeddings, knn_mean, pair_rows, pair_cols, pair_count, start_block):
    unit = unit_rows(embeddings)
    slots = pair_rows.shape[2]
    live = (jnp.arange(slots, dtype=jnp.int32)[None, None, :] < pair_count[:, :, None]).reshape(-1)
    flat_rows = pair_rows.reshape(-1).astype(jnp.int32)
    flat_cols = pair_cols.reshape(-1).astype(jnp.int32)
    total_rows = embeddings.shape[0]
    vector = start_block
    for sweep in range(ITERS):
        narrow = vector.astype(jnp.bfloat16)

        def accumulate(state, item):
            row_block, col_block, active = item

            def apply(inner):
                vector_acc, degree_acc = inner
                row_unit = lax.dynamic_slice_in_dim(unit, row_block * BLOCK, BLOCK, 0)
                col_unit = lax.dynamic_slice_in_dim(unit, col_block * BLOCK, BLOCK, 0)
                row_mean = lax.dynamic_slice_in_dim(knn_mean, row_block * BLOCK, BLOCK, 0)
                col_mean = lax.dynamic_slice_in_dim(knn_mean, col_block * BLOCK, BLOCK, 0)
                affinity = make_affinity(row_unit, col_unit, row_mean, col_mean, row_block, col_block)
                degree_acc = add_block(degree_acc, lax.optimization_barrier(jnp.sum(affinity.astype(jnp.float32), axis=1))[None, :], row_block)
                source = lax.dynamic_slice_in_dim(narrow, col_block * BLOCK, BLOCK, 1)
                product = lax.dot_general(source.astype(jnp.float32), affinity.astype(jnp.float32), (((1,), (1,)), ((), ())), preferred_element_type=jnp.float32)
                vector_acc = add_block(vector_acc, product, row_block)
                return (vector_acc, degree_acc)
            return (lax.cond(active, apply, lambda inner: inner, state), None)
        init = (jnp.zeros((K, total_rows), jnp.float32), jnp.zeros((1, total_rows), jnp.float32))
        (summed, degree), _ = lax.scan(accumulate, init, (flat_rows, flat_cols, live))
        smoothed = summed / degree
        gram = jnp.dot(smoothed.astype(jnp.float32), smoothed.T.astype(jnp.float32), precision=lax.Precision.HIGHEST, preferred_element_type=jnp.float32) / total_rows
        lower = jnp.linalg.cholesky(gram)
        vector = jax.scipy.linalg.solve_triangular(lower, smoothed, lower=True)
    return vector
```

```python
import functools

import jax
import jax.numpy as jnp
from jax import lax
from jax.experimental import pallas as pl
from jax.experimental.pallas import tpu as pltpu
from jax.sharding import PartitionSpec as P

MESH = pl.DeviceIdType.MESH
NY, NC = 4, 2
K = 64
KA = 80
KD = 72
sharpness = 10.0
epsilon = 1e-06

F32 = jnp.float32
BF16 = jnp.bfloat16
HIGH = lax.Precision.HIGHEST


def dot_nt(a, b, precision=None):
    return lax.dot_general(
        a, b, (((1,), (1,)), ((), ())), precision=precision, preferred_element_type=F32
    )


def dot_nn(a, b, precision=None):
    return jnp.dot(a, b, precision=precision, preferred_element_type=F32)


def normalize(src, dst, rows):
    width = src.shape[1]
    chunk = 32

    def body(c, carry):
        at = pl.ds(pl.multiple_of(c * chunk, chunk), chunk)
        values = src[at, :].astype(F32)
        square = jnp.sum(values * values, axis=1, keepdims=True) * (1.0 / width)
        scale = lax.rsqrt(square + epsilon) * (1.0 / width**0.5)
        dst[at, :] = (values * scale).astype(BF16)
        return carry

    lax.fori_loop(0, rows // chunk, body, 0)


def inverse_factor(matrix):
    lane = lax.broadcasted_iota(jnp.int32, (8, 2 * K), 1)
    row8 = lax.broadcasted_iota(jnp.int32, (8, 2 * K), 0)
    work = [
        jnp.where(lane < K, matrix[8 * m : 8 * m + 8, :], (lane - K == row8 + 8 * m).astype(F32))
        for m in range(K // 8)
    ]
    pivots = [None] * (K // 8)
    for k in range(K):
        m0, s = k // 8, k % 8
        row = jnp.broadcast_to(work[m0][s : s + 1, :], (8, 2 * K))
        pivot = jnp.broadcast_to(row[:, k : k + 1], (8, 2 * K))
        ratio = row / pivot
        here = row8 == s
        pivots[m0] = pivot if pivots[m0] is None else jnp.where(here, pivot, pivots[m0])
        for m in range(m0, K // 8):
            column = jnp.broadcast_to(work[m][:, k : k + 1], (8, 2 * K))
            update = column * ratio
            if m == m0:
                if s == 7:
                    continue
                update = jnp.where(row8 > s, update, 0.0)
            work[m] = work[m] - update
    done = [work[m] * lax.rsqrt(pivots[m]) for m in range(K // 8)]
    return jnp.concatenate(done, axis=0)[:, K:]


def kernel(
    nz, ny, nc, nx, total_rows,
    emb, knn, prow, pcol, pcnt, start,
    out,
    emb_v, unit, emb_h, unit_h, km, km_h, mcol, v0, v0_h, sc, aff, part1, part2, rs1, rs2,
    nar, nar_h, mask, mask_x, msum, yall, gpart, ga, gsum, gb, gsum2, gc, gfull,
    local_sem, emb_s, emb_r, km_s, km_r, v0_s, v0_r, mask_s, mask_r,
    rs1_s, rs1_r, rs2_s, rs2_r, nar_s, nar_r, y_s, y_r,
    ga_s, ga_r, gb_s, gb_r, gc_s, gc_r, gd_s, gd_r,
):
    g = lax.axis_index("rows")
    x = lax.axis_index("cols")
    rows = nz * ny * nc
    core = g % nc
    y = (g // nc) % ny
    z = g // (nc * ny)
    block = emb_h.shape[1]
    here = emb_v.shape[0]
    blocks = here // block
    parts = nc * nx

    def at(dz=0, dy=0, dc=0, dx=0):
        row = (((z + dz) % nz) * ny + (y + dy) % ny) * nc + (core + dc) % nc
        return (row, (x + dx) % nx)

    sides = [((g + 1) % rows, x), ((g + rows - 1) % rows, x)]
    near = [(e // nx, e % nx) for e in range(1, parts)]
    xpeers = [at(dx=d) for d in range(1, nx)]
    npeers = [at(dc=dc, dx=dx) for dc, dx in near]
    ypeers = [at(dy=d) for d in range(1, ny)]
    zpeers = [at(dz=d) for d in range(1, nz)]

    barrier = pltpu.get_barrier_semaphore()
    everyone = sides + npeers + ypeers + zpeers
    for peer in everyone:
        pl.semaphore_signal(barrier, inc=1, device_id=peer, device_id_type=MESH)

    started = []

    def remote(src, dst, ssem, rsem, peer):
        return pltpu.make_async_remote_copy(
            src_ref=src, dst_ref=dst, send_sem=ssem, recv_sem=rsem,
            device_id=peer, device_id_type=MESH,
        )

    def send(src, dst, ssem, rsem, peer):
        copy = remote(src, dst, ssem, rsem, peer)
        copy.start()
        started.append(copy)
        return copy

    own = pl.ds(pl.multiple_of(x * block, block), block)
    for r in range(blocks):
        pltpu.make_async_copy(
            emb.at[pl.ds(r * block, block)], emb_v.at[pl.ds(r * block, block)], local_sem.at[r]
        ).start()
    load_v = pltpu.make_async_copy(start.at[:, own], v0, local_sem.at[blocks])
    load_v.start()

    slots = prow.shape[-1]
    spot = (prow[0] - g * blocks) * (3 * blocks) + (pcol[0] - (g - 1) * blocks)
    live = lax.broadcasted_iota(jnp.int32, (1, slots), 1) < pcnt[...]
    spot = jnp.where(live, spot, -1)
    hit = lax.broadcasted_iota(jnp.int32, (mask.shape[0], slots), 0) == spot
    mask[...] = jnp.broadcast_to(
        jnp.sum(jnp.where(hit, 1.0, 0.0), axis=1, keepdims=True), mask.shape
    )
    means = knn[...].astype(F32)
    for r in range(blocks):
        km[r] = jnp.broadcast_to(means[:, r * block : (r + 1) * block], (8, block))

    pl.semaphore_wait(barrier, len(everyone))

    for h, peer in enumerate(sides):
        send(km.at[x], km_h.at[h], km_s.at[h], km_r.at[h], peer)
    for h, peer in enumerate(sides):
        send(start.at[:, own], v0_h.at[h], v0_s.at[h], v0_r.at[h], peer)
    for h, peer in enumerate(sides):
        send(emb.at[own], emb_h.at[h], emb_s.at[h], emb_r.at[h], peer)
    masks = [
        send(mask, mask_x.at[d], mask_s.at[d], mask_r.at[d], peer) for d, peer in enumerate(xpeers)
    ]

    for r in range(blocks):
        where = pl.ds(r * block, block)
        pltpu.make_async_copy(emb.at[where], emb_v.at[where], local_sem.at[r]).wait()
        normalize(emb_v.at[where], unit.at[where], block)
    lane = lax.broadcasted_iota(jnp.int32, (block, block), 1)
    line = lax.broadcasted_iota(jnp.int32, (block, block), 0)
    eye = jnp.where(lane == line, 1.0, 0.0).astype(BF16)
    for r in range(blocks):
        wide = jnp.broadcast_to(km[r, 0:1, :], (128, block)).astype(BF16)
        mcol[pl.ds(r * block, block), :] = dot_nt(eye, wide)

    chunk = 64

    def affinity(slot, unit_col, mean_row, diagonal):
        sc[...] = dot_nt(unit[...], unit_col)

        def body(c, carry):
            rows_at = pl.ds(pl.multiple_of(c * chunk, chunk), chunk)
            side = mcol[rows_at, :]
            denom = 0.5 * (jnp.concatenate([side] * (block // 128), axis=1) + mean_row)
            weights = jnp.exp(sharpness * sc[rows_at, :] / denom)
            if diagonal:
                a = lax.broadcasted_iota(jnp.int32, (chunk, block), 0) + c * chunk
                b = lax.broadcasted_iota(jnp.int32, (chunk, block), 1) + x * block
                weights = jnp.where(a == b, 0.0, weights)
            aff[slot, rows_at, :] = weights.astype(BF16)
            return carry

        lax.fori_loop(0, here // chunk, body, 0)

    def product(slot, window, source, part, first):
        for r in range(blocks):
            live_pair = msum[pl.ds(r * 3 * blocks + window * blocks + x, 1), :][:, 0:1]
            piece = dot_nt(source, aff[slot, pl.ds(r * block, block), :]) * live_pair
            part[r, pl.ds(0, piece.shape[0]), :] = (
                piece if first else part[r, pl.ds(0, piece.shape[0]), :] + piece
            )

    tail = lax.broadcasted_iota(jnp.int32, (KA - K, block), 0)
    ones = jnp.where(tail == 0, 1.0, 0.0)

    def widened(values):
        return jnp.concatenate([values, ones], axis=0).astype(BF16)

    affinity(2, unit[own, :], km[x, 0:1, :], True)
    for c in masks:
        c.wait_recv()
    msum[...] = mask[...]
    for d in range(nx - 1):
        msum[...] += mask_x[d]
    load_v.wait()
    product(2, 1, widened(v0[...]), part1, True)

    def side(step, carry):
        h = (core + 1 + step) % 2
        remote(km.at[x], km_h.at[h], km_s.at[h], km_r.at[h], sides[0]).wait_recv()
        remote(start.at[:, own], v0_h.at[h], v0_s.at[h], v0_r.at[h], sides[0]).wait_recv()
        remote(emb.at[own], emb_h.at[h], emb_s.at[h], emb_r.at[h], sides[0]).wait_recv()
        normalize(emb_h.at[h], unit_h, block)
        affinity(h, unit_h[...], km_h[h, 0:1, :], False)
        product(h, 2 * h, widened(v0_h[h]), part1, False)
        return carry

    lax.fori_loop(0, 2, side, 0)

    scatter = [
        send(part1.at[(x + d) % nx, pl.ds(0, KD)], rs1.at[d - 1], rs1_s.at[d - 1], rs1_r.at[d - 1], peer)
        for d, peer in zip(range(1, nx), xpeers)
    ]
    for c in scatter:
        c.wait_recv()
    total = part1[x, pl.ds(0, KD), :]
    for d in range(nx - 1):
        total = total + rs1[d]
    degree = total[K : K + 1, :]
    smoothed1 = total[:K, :] / degree
    nar[...] = smoothed1.astype(BF16)

    narrow = [send(nar, nar_h.at[h], nar_s.at[h], nar_r.at[h], peer) for h, peer in enumerate(sides)]
    gram1 = dot_nt(smoothed1, smoothed1, HIGH) * (1.0 / total_rows)
    product(2, 1, nar[...], part2, True)
    for c in narrow:
        c.wait_recv()
    for h in range(2):
        product(h, 2 * h, nar_h[h], part2, False)
    scatter = [
        send(part2.at[(x + d) % nx], rs2.at[d - 1], rs2_s.at[d - 1], rs2_r.at[d - 1], peer)
        for d, peer in zip(range(1, nx), xpeers)
    ]
    for c in scatter:
        c.wait_recv()
    total = part2[x]
    for d in range(nx - 1):
        total = total + rs2[d]
    smoothed2 = total / degree
    yall[0] = smoothed2
    gather = [
        send(yall.at[0], yall.at[d], y_s.at[d - 1], y_r.at[d - 1], peer)
        for d, peer in zip(range(1, nx), xpeers)
    ]

    gram2 = dot_nt(smoothed2, smoothed2, HIGH) * (1.0 / total_rows)
    both = jnp.concatenate([gram1, gram2], axis=1)
    height = K // parts
    for p in range(parts):
        gpart[p] = both[p * height : (p + 1) * height, :]
    copies = [
        send(
            gpart.at[((core + dc) % nc) * nx + (x + dx) % nx], ga.at[e], ga_s.at[e], ga_r.at[e], peer
        )
        for e, ((dc, dx), peer) in enumerate(zip(near, npeers))
    ]
    for c in copies:
        c.wait_recv()
    total = gpart[core * nx + x]
    for e in range(parts - 1):
        total = total + ga[e]
    gsum[...] = total
    copies = [
        send(gsum, gb.at[d], gb_s.at[d], gb_r.at[d], peer) for d, peer in enumerate(ypeers)
    ]
    for c in copies:
        c.wait_recv()
    for d in range(ny - 1):
        total = total + gb[d]
    gsum2[...] = total
    copies = [
        send(gsum2, gc.at[d], gc_s.at[d], gc_r.at[d], peer) for d, peer in enumerate(zpeers)
    ]
    for c in copies:
        c.wait_recv()
    for d in range(nz - 1):
        total = total + gc[d]
    gfull[0] = total
    copies = [
        send(gfull.at[0], gfull.at[e + 1], gd_s.at[e], gd_r.at[e], peer)
        for e, peer in enumerate(npeers)
    ]
    for c in copies:
        c.wait_recv()
    gram = jnp.concatenate(
        [gfull[((core + nc - p // nx) % nc) * nx + (x + nx - p % nx) % nx] for p in range(parts)],
        axis=0,
    )

    first = inverse_factor(gram)
    inner = dot_nt(dot_nn(first, gram[:, K:], HIGH), first, HIGH)
    second = inverse_factor(jnp.concatenate([inner, inner], axis=1))
    whiten = dot_nn(second, first, HIGH)
    for c in gather:
        c.wait_recv()
    for p in range(nx):
        out[:, pl.ds(p * block, block)] = dot_nn(whiten, yall[(x + nx - p) % nx], HIGH)
    for c in started:
        c.wait_send()


def solution(mesh):
    nx = mesh.shape["cols"]
    groups = mesh.shape["rows"]
    nz = groups // (NY * NC)
    parts = NC * nx

    def local(embeddings, knn_mean, pair_rows, pair_cols, pair_count, start_block):
        here, width = embeddings.shape
        block = here // nx
        height = K // parts
        dma = pltpu.SemaphoreType.DMA
        vmem = pl.BlockSpec(memory_space=pltpu.VMEM)
        hbm = pl.BlockSpec(memory_space=pl.ANY)
        return pl.pallas_call(
            functools.partial(kernel, nz, NY, NC, nx, here * groups),
            out_shape=jax.ShapeDtypeStruct((K, here), F32),
            in_specs=[hbm, vmem, vmem, vmem, vmem, hbm],
            out_specs=vmem,
            scratch_shapes=[
                pltpu.VMEM((here, width), BF16),
                pltpu.VMEM((here, width), BF16),
                pltpu.VMEM((2, block, width), BF16),
                pltpu.VMEM((block, width), BF16),
                pltpu.VMEM((nx, 8, block), F32),
                pltpu.VMEM((2, 8, block), F32),
                pltpu.VMEM((here, 128), F32),
                pltpu.VMEM((K, block), F32),
                pltpu.VMEM((2, K, block), F32),
                pltpu.VMEM((here, block), F32),
                pltpu.VMEM((3, here, block), BF16),
                pltpu.VMEM((nx, KA, block), F32),
                pltpu.VMEM((nx, K, block), F32),
                pltpu.VMEM((nx - 1, KD, block), F32),
                pltpu.VMEM((nx - 1, K, block), F32),
                pltpu.VMEM((K, block), BF16),
                pltpu.VMEM((2, K, block), BF16),
                pltpu.VMEM((3 * nx * nx, 128), F32),
                pltpu.VMEM((nx - 1, 3 * nx * nx, 128), F32),
                pltpu.VMEM((3 * nx * nx, 128), F32),
                pltpu.VMEM((nx, K, block), F32),
                pltpu.VMEM((parts, height, 2 * K), F32),
                pltpu.VMEM((parts - 1, height, 2 * K), F32),
                pltpu.VMEM((height, 2 * K), F32),
                pltpu.VMEM((NY - 1, height, 2 * K), F32),
                pltpu.VMEM((height, 2 * K), F32),
                pltpu.VMEM((nz - 1, height, 2 * K), F32),
                pltpu.VMEM((parts, height, 2 * K), F32),
                dma((nx + 1,)),
                dma((2,)), dma((2,)), dma((2,)), dma((2,)), dma((2,)), dma((2,)),
                dma((nx - 1,)), dma((nx - 1,)),
                dma((nx - 1,)), dma((nx - 1,)),
                dma((nx - 1,)), dma((nx - 1,)),
                dma((2,)), dma((2,)),
                dma((nx - 1,)), dma((nx - 1,)),
                dma((parts - 1,)), dma((parts - 1,)),
                dma((NY - 1,)), dma((NY - 1,)),
                dma((nz - 1,)), dma((nz - 1,)),
                dma((parts - 1,)), dma((parts - 1,)),
            ],
            compiler_params=pltpu.CompilerParams(collective_id=0, has_side_effects=True),
        )(embeddings, knn_mean.reshape(1, here), pair_rows, pair_cols, pair_count, start_block)

    in_specs = (
        P("rows", None),
        P("rows"),
        P("rows", "cols", None),
        P("rows", "cols", None),
        P("rows", "cols"),
        P(None, "rows"),
    )
    out_specs = P(None, "rows")
    return jax.shard_map(local, mesh=mesh, in_specs=in_specs, out_specs=out_specs, check_vma=False)
```

```python
import functools

import jax
import jax.numpy as jnp
from jax import lax
from jax.experimental import pallas as pl
from jax.experimental.pallas import tpu as pltpu
from jax.sharding import PartitionSpec as P

MESH = pl.DeviceIdType.MESH
NY, NC = 4, 2
K = 64
KA = 80
KD = 72
PANEL = 8
sharpness = 10.0
epsilon = 1e-06

F32 = jnp.float32
BF16 = jnp.bfloat16
HIGH = lax.Precision.HIGHEST


def dot_nt(a, b, precision=None):
    return lax.dot_general(
        a, b, (((1,), (1,)), ((), ())), precision=precision, preferred_element_type=F32
    )


def dot_nn(a, b, precision=None):
    return jnp.dot(a, b, precision=precision, preferred_element_type=F32)


def normalize(src, dst, rows):
    width = src.shape[1]
    chunk = 64

    def body(c, carry):
        at = pl.ds(pl.multiple_of(c * chunk, chunk), chunk)
        values = src[at, :].astype(F32)
        square = jnp.sum(values * values, axis=1, keepdims=True) * (1.0 / width)
        scale = lax.rsqrt(square + epsilon) * (1.0 / width**0.5)
        dst[at, :] = (values * scale).astype(BF16)
        return carry

    lax.fori_loop(0, rows // chunk, body, 0, unroll=4)


def inverse_factor(matrix):
    wide = (8, 2 * K)
    lane = lax.broadcasted_iota(jnp.int32, wide, 1)
    row8 = lax.broadcasted_iota(jnp.int32, wide, 0)
    tall = K // 8

    def spread(values, k):
        return jnp.broadcast_to(values[:, k : k + 1], wide)

    blocks = [matrix[8 * m : 8 * m + 8, :] for m in range(tall)]
    marks = [lane == row8 + 8 * m for m in range(tall)]
    diagonals = [jnp.where(marks[m], blocks[m], 0.0) for m in range(tall)]
    along = sum(diagonals[1:], diagonals[0])
    along = jnp.broadcast_to(jnp.sum(along, axis=0, keepdims=True), wide)
    along = lax.rsqrt(jnp.where(lane < K, along, 1.0))
    work = []
    for m in range(tall):
        down = lax.rsqrt(jnp.broadcast_to(jnp.sum(diagonals[m], axis=1, keepdims=True), wide))
        right = jnp.where(lane - K == row8 + 8 * m, down, 0.0)
        work.append(jnp.where(lane < K, blocks[m] * down * along, right))
    done = []
    for m0 in range(tall):
        k = m0 * PANEL
        rows = [jnp.broadcast_to(work[m0][t : t + 1, :], wide) for t in range(PANEL)]
        a = {(t, u): spread(rows[t], k + u) for t in range(PANEL) for u in range(t, PANEL)}
        low, inv, pivot = {}, [None] * PANEL, [None] * PANEL
        for t in range(0, PANEL, 2):
            p, q = a[t, t], a[t, t + 1]
            det = p * a[t + 1, t + 1] - q * q
            inv[t] = 1.0 / p
            inv[t + 1] = p * (1.0 / det)
            pivot[t], pivot[t + 1] = p, det * inv[t]
            low[t + 1, t] = q * inv[t]
            for u in range(t + 2, PANEL):
                low[u, t] = a[t, u] * inv[t]
                a[t + 1, u] = a[t + 1, u] - low[t + 1, t] * a[t, u]
                low[u, t + 1] = a[t + 1, u] * inv[t + 1]
            for u in range(t + 2, PANEL):
                for v in range(u, PANEL):
                    a[u, v] = a[u, v] - low[u, t] * a[t, v] - low[u, t + 1] * a[t + 1, v]
        for t in range(1, PANEL):
            for u in range(t):
                rows[t] = rows[t] - low[t, u] * rows[u]
        scaled = [rows[t] * inv[t] for t in range(PANEL)]
        for m in range(m0 + 1, tall):
            column = [spread(work[m], k + t) for t in range(PANEL)]
            for t in range(1, PANEL):
                for u in range(t):
                    column[t] = column[t] - low[t, u] * column[u]
            for t in range(PANEL):
                work[m] = work[m] - column[t] * scaled[t]
        reduced, pivots = rows[0], pivot[0]
        for t in range(1, PANEL):
            reduced = jnp.where(row8 == t, rows[t], reduced)
            pivots = jnp.where(row8 == t, pivot[t], pivots)
        done.append(reduced * lax.rsqrt(pivots))
    return jnp.concatenate(done, axis=0)[:, K:]


def kernel(
    nz, ny, nc, nx, total_rows,
    emb, knn, prow, pcol, pcnt, start,
    out,
    emb_v, unit, emb_h, unit_h, km, km_h, mcol, v0, v0_h, aff, part1, half1, part2, rs1, rs1_d, rs2,
    nar, nar_h, mask, mask_x, msum, yall, gpart, ga, gsum, gb, gsum2, gc, gfull,
    local_sem, emb_s, emb_r, km_s, km_r, v0_s, v0_r, mask_s, mask_r,
    rs1_s, rs1_r, rsd_s, rsd_r, rs2_s, rs2_r, nar_s, nar_r, y_s, y_r,
    ga_s, ga_r, gb_s, gb_r, gc_s, gc_r, gd_s, gd_r, reach_sem,
):
    g = lax.axis_index("rows")
    x = lax.axis_index("cols")
    rows = nz * ny * nc
    core = g % nc
    y = (g // nc) % ny
    z = g // (nc * ny)
    block = emb_h.shape[1]
    here = emb_v.shape[0]
    blocks = here // block
    parts = nc * nx

    def at(dz=0, dy=0, dc=0, dx=0):
        row = (((z + dz) % nz) * ny + (y + dy) % ny) * nc + (core + dc) % nc
        return (row, (x + dx) % nx)

    sides = [((g + 1) % rows, x), ((g + rows - 1) % rows, x)]
    near = [(e // nx, e % nx) for e in range(1, parts)]
    xpeers = [at(dx=d) for d in range(1, nx)]
    npeers = [at(dc=dc, dx=dx) for dc, dx in near]
    ypeers = [at(dy=d) for d in range(1, ny)]
    zpeers = [at(dz=d) for d in range(1, nz)]

    barrier = pltpu.get_barrier_semaphore()
    zreach = [d for d in range(1, nz) if min(d, nz - d) <= 2]
    rounds = []
    while 2 * 2 ** len(rounds) < nz // 2:
        rounds.append(2 * 2 ** len(rounds))
    everyone = sides + npeers + ypeers + [at(dz=d) for d in zreach]
    for peer in everyone:
        pl.semaphore_signal(barrier, inc=1, device_id=peer, device_id_type=MESH)

    started = []

    def remote(src, dst, ssem, rsem, peer):
        return pltpu.make_async_remote_copy(
            src_ref=src, dst_ref=dst, send_sem=ssem, recv_sem=rsem,
            device_id=peer, device_id_type=MESH,
        )

    def send(src, dst, ssem, rsem, peer):
        copy = remote(src, dst, ssem, rsem, peer)
        copy.start()
        started.append(copy)
        return copy

    own = pl.ds(pl.multiple_of(x * block, block), block)
    for r in range(blocks):
        pltpu.make_async_copy(
            emb.at[pl.ds(r * block, block)], emb_v.at[pl.ds(r * block, block)], local_sem.at[r]
        ).start()
    load_v = pltpu.make_async_copy(start.at[:, own], v0, local_sem.at[blocks])
    load_v.start()

    slots = prow.shape[-1]
    spot = (prow[0] - g * blocks) * (3 * blocks) + (pcol[0] - (g - 1) * blocks)
    live = lax.broadcasted_iota(jnp.int32, (1, slots), 1) < pcnt[...]
    spot = jnp.where(live, spot, -1)
    hit = lax.broadcasted_iota(jnp.int32, (mask.shape[0], slots), 0) == spot
    mask[...] = jnp.broadcast_to(
        jnp.sum(jnp.where(hit, 1.0, 0.0), axis=1, keepdims=True), mask.shape
    )
    means = knn[...].astype(F32).reshape(1, here)
    for r in range(blocks):
        km[r] = jnp.broadcast_to(means[:, r * block : (r + 1) * block], (8, block))

    def reach_signal(n):
        for dz in (rounds[n], -rounds[n]):
            pl.semaphore_signal(
                reach_sem.at[n], inc=1, device_id=at(dz=nz + dz), device_id_type=MESH
            )

    pl.semaphore_wait(barrier, len(everyone))

    for h, peer in enumerate(sides):
        send(km.at[x], km_h.at[h], km_s.at[h], km_r.at[h], peer)
    for h, peer in enumerate(sides):
        send(emb.at[own], emb_h.at[h], emb_s.at[h], emb_r.at[h], peer)
    for h, peer in enumerate(sides):
        send(start.at[:, own], v0_h.at[h], v0_s.at[h], v0_r.at[h], peer)
    masks = [
        send(mask, mask_x.at[d], mask_s.at[d], mask_r.at[d], peer) for d, peer in enumerate(xpeers)
    ]

    if rounds:
        reach_signal(0)

    for r in range(blocks):
        where = pl.ds(r * block, block)
        pltpu.make_async_copy(emb.at[where], emb_v.at[where], local_sem.at[r]).wait()
        normalize(emb_v.at[where], unit.at[where], block)
    lane = lax.broadcasted_iota(jnp.int32, (block, block), 1)
    line = lax.broadcasted_iota(jnp.int32, (block, block), 0)
    eye = jnp.where(lane == line, 1.0, 0.0).astype(BF16)
    for r in range(blocks):
        wide = jnp.broadcast_to(km[r, 0:1, :], (128, block)).astype(BF16)
        mcol[pl.ds(r * block, block), :] = dot_nt(eye, wide)

    def affinity(slot, unit_col, mean_row, diagonal):
        for r in range(blocks):
            rows_at = pl.ds(r * block, block)
            scores = dot_nt(unit[rows_at, :], unit_col)
            side = jnp.concatenate([mcol[rows_at, :]] * (block // 128), axis=1)
            denom = 0.5 * (side + mean_row)
            weights = jnp.exp(sharpness * scores / denom)
            if diagonal:
                weights = jnp.where((lane == line) & (x == r), 0.0, weights)
            aff[slot, rows_at, :] = weights.astype(BF16)

    def product(slot, window, source, part, first):
        for r in range(blocks):
            live_pair = msum[pl.ds(r * 3 * blocks + window * blocks + x, 1), :][:, 0:1]
            piece = dot_nt(source, aff[slot, pl.ds(r * block, block), :]) * live_pair
            part[r, pl.ds(0, piece.shape[0]), :] = (
                piece if first else part[r, pl.ds(0, piece.shape[0]), :] + piece
            )

    tail = lax.broadcasted_iota(jnp.int32, (KA - K, block), 0)
    ones = jnp.where(tail == 0, 1.0, 0.0)

    def widened(values):
        return jnp.concatenate([values, ones], axis=0).astype(BF16)

    affinity(2, unit[own, :], km[x, 0:1, :], True)
    for c in masks:
        c.wait_recv()
    msum[...] = mask[...]
    for d in range(nx - 1):
        msum[...] += mask_x[d]
    load_v.wait()
    product(2, 1, widened(v0[...]), part1, True)

    for n in range(len(rounds)):
        pl.semaphore_wait(reach_sem.at[n], 2)
        if n + 1 < len(rounds):
            reach_signal(n + 1)

    def side(step, carry):
        h = (core + 1 + step) % 2
        remote(km.at[x], km_h.at[h], km_s.at[h], km_r.at[h], sides[0]).wait_recv()
        remote(emb.at[own], emb_h.at[h], emb_s.at[h], emb_r.at[h], sides[0]).wait_recv()
        normalize(emb_h.at[h], unit_h, block)
        affinity(h, unit_h[...], km_h[h, 0:1, :], False)
        remote(start.at[:, own], v0_h.at[h], v0_s.at[h], v0_r.at[h], sides[0]).wait_recv()
        product(h, 2 * h, widened(v0_h[h]), part1, False)
        return carry

    lax.fori_loop(0, 2, side, 0)

    for r in range(blocks):
        half1[r] = part1[r, pl.ds(0, K), :].astype(BF16)
    scatter = []
    for d, peer in zip(range(1, nx), xpeers):
        p, e = (x + d) % nx, d - 1
        scatter.append(send(half1.at[p], rs1.at[e], rs1_s.at[e], rs1_r.at[e], peer))
        scatter.append(
            send(part1.at[p, pl.ds(K, KD - K)], rs1_d.at[e], rsd_s.at[e], rsd_r.at[e], peer)
        )
    for c in scatter:
        c.wait_recv()
    total = part1[x, pl.ds(0, K), :]
    degree = part1[x, pl.ds(K, KD - K), :]
    for d in range(nx - 1):
        total = total + rs1[d].astype(F32)
        degree = degree + rs1_d[d]
    degree = degree[0:1, :]
    smoothed1 = total / degree
    nar[...] = smoothed1.astype(BF16)

    height = K // parts
    me = core * nx + x

    def gram_a(q, smoothed):
        gram = dot_nt(smoothed, smoothed, HIGH) * (1.0 / total_rows)
        gram = jnp.concatenate([gram, jnp.zeros_like(gram)], axis=1)
        for p in range(parts):
            gpart[q, p] = gram[p * height : (p + 1) * height, :]
        return [
            send(
                gpart.at[q, ((core + dc) % nc) * nx + (x + dx) % nx],
                ga.at[q, e], ga_s.at[q, e], ga_r.at[q, e], peer,
            )
            for e, ((dc, dx), peer) in enumerate(zip(near, npeers))
        ]

    def gram_b(q, copies):
        for c in copies:
            c.wait_recv()
        total = gpart[q, me]
        for e in range(parts - 1):
            total = total + ga[q, e]
        gsum[q] = total
        return [
            send(gsum.at[q], gb.at[q, d], gb_s.at[q, d], gb_r.at[q, d], peer)
            for d, peer in enumerate(ypeers)
        ]

    def gram_c(q, copies):
        for c in copies:
            c.wait_recv()
        total = gsum[q]
        for d in range(ny - 1):
            total = total + gb[q, d]
        gsum2[q] = total
        return [
            send(gsum2.at[q], gc.at[q, d], gc_s.at[q, d], gc_r.at[q, d], peer)
            for d, peer in enumerate(zpeers)
        ]

    def gram_d(q, copies):
        for c in copies:
            c.wait_recv()
        total = gsum2[q]
        for d in range(nz - 1):
            total = total + gc[q, d]
        gfull[q, 0] = total
        return [
            send(gfull.at[q, 0], gfull.at[q, e + 1], gd_s.at[q, e], gd_r.at[q, e], peer)
            for e, peer in enumerate(npeers)
        ]

    def gram_whole(q, copies):
        for c in copies:
            c.wait_recv()
        pieces = [
            gfull[q, ((core + nc - p // nx) % nc) * nx + (x + nx - p % nx) % nx]
            for p in range(parts)
        ]
        return jnp.concatenate(pieces, axis=0)

    narrow = [send(nar, nar_h.at[h], nar_s.at[h], nar_r.at[h], peer) for h, peer in enumerate(sides)]
    sum1 = gram_a(0, smoothed1)
    product(2, 1, nar[...], part2, True)
    for c in narrow:
        c.wait_recv()
    for h in range(2):
        product(h, 2 * h, nar_h[h], part2, False)
    scatter = [
        send(part2.at[(x + d) % nx], rs2.at[d - 1], rs2_s.at[d - 1], rs2_r.at[d - 1], peer)
        for d, peer in zip(range(1, nx), xpeers)
    ]
    sum1 = gram_c(0, gram_b(0, sum1))
    for c in scatter:
        c.wait_recv()
    total = part2[x]
    for d in range(nx - 1):
        total = total + rs2[d]
    smoothed2 = total / degree
    yall[0] = smoothed2
    sum2 = gram_b(1, gram_a(1, smoothed2))
    gather = [
        send(yall.at[0], yall.at[d], y_s.at[d - 1], y_r.at[d - 1], peer)
        for d, peer in zip(range(1, nx), xpeers)
    ]
    sum2 = gram_c(1, sum2)
    first = inverse_factor(gram_whole(0, gram_d(0, sum1)))
    gram = gram_whole(1, gram_d(1, sum2))

    inner = dot_nt(dot_nn(first, gram[:, :K], HIGH), first, HIGH)
    second = inverse_factor(jnp.concatenate([inner, inner], axis=1))
    whiten = dot_nn(second, first, HIGH)
    for c in gather:
        c.wait_recv()
    for p in range(nx):
        out[:, pl.ds(p * block, block)] = dot_nn(whiten, yall[(x + nx - p) % nx], HIGH)
    for c in started:
        c.wait_send()


def solution(mesh):
    nx = mesh.shape["cols"]
    groups = mesh.shape["rows"]
    nz = groups // (NY * NC)
    parts = NC * nx

    def local(embeddings, knn_mean, pair_rows, pair_cols, pair_count, start_block):
        here, width = embeddings.shape
        block = here // nx
        height = K // parts
        dma = pltpu.SemaphoreType.DMA
        vmem = pl.BlockSpec(memory_space=pltpu.VMEM)
        hbm = pl.BlockSpec(memory_space=pl.ANY)
        return pl.pallas_call(
            functools.partial(kernel, nz, NY, NC, nx, here * groups),
            out_shape=jax.ShapeDtypeStruct((K, here), F32),
            in_specs=[hbm, vmem, vmem, vmem, vmem, hbm],
            out_specs=vmem,
            scratch_shapes=[
                pltpu.VMEM((here, width), BF16),
                pltpu.VMEM((here, width), BF16),
                pltpu.VMEM((2, block, width), BF16),
                pltpu.VMEM((block, width), BF16),
                pltpu.VMEM((nx, 8, block), F32),
                pltpu.VMEM((2, 8, block), F32),
                pltpu.VMEM((here, 128), F32),
                pltpu.VMEM((K, block), F32),
                pltpu.VMEM((2, K, block), F32),
                pltpu.VMEM((3, here, block), BF16),
                pltpu.VMEM((nx, KA, block), F32),
                pltpu.VMEM((nx, K, block), BF16),
                pltpu.VMEM((nx, K, block), F32),
                pltpu.VMEM((nx - 1, K, block), BF16),
                pltpu.VMEM((nx - 1, KD - K, block), F32),
                pltpu.VMEM((nx - 1, K, block), F32),
                pltpu.VMEM((K, block), BF16),
                pltpu.VMEM((2, K, block), BF16),
                pltpu.VMEM((3 * nx * nx, 128), F32),
                pltpu.VMEM((nx - 1, 3 * nx * nx, 128), F32),
                pltpu.VMEM((3 * nx * nx, 128), F32),
                pltpu.VMEM((nx, K, block), F32),
                pltpu.VMEM((2, parts, height, 2 * K), F32),
                pltpu.VMEM((2, parts - 1, height, 2 * K), F32),
                pltpu.VMEM((2, height, 2 * K), F32),
                pltpu.VMEM((2, NY - 1, height, 2 * K), F32),
                pltpu.VMEM((2, height, 2 * K), F32),
                pltpu.VMEM((2, nz - 1, height, 2 * K), F32),
                pltpu.VMEM((2, parts, height, 2 * K), F32),
                dma((nx + 1,)),
                dma((2,)), dma((2,)), dma((2,)), dma((2,)), dma((2,)), dma((2,)),
                dma((nx - 1,)), dma((nx - 1,)),
                dma((nx - 1,)), dma((nx - 1,)), dma((nx - 1,)), dma((nx - 1,)),
                dma((nx - 1,)), dma((nx - 1,)),
                dma((2,)), dma((2,)),
                dma((nx - 1,)), dma((nx - 1,)),
                dma((2, parts - 1)), dma((2, parts - 1)),
                dma((2, NY - 1)), dma((2, NY - 1)),
                dma((2, nz - 1)), dma((2, nz - 1)),
                dma((2, parts - 1)), dma((2, parts - 1)),
                pltpu.SemaphoreType.REGULAR((4,)),
            ],
            compiler_params=pltpu.CompilerParams(collective_id=0, has_side_effects=True),
        )(embeddings, knn_mean, pair_rows, pair_cols, pair_count, start_block)

    in_specs = (
        P("rows", None),
        P("rows"),
        P("rows", "cols", None),
        P("rows", "cols", None),
        P("rows", "cols"),
        P(None, "rows"),
    )
    out_specs = P(None, "rows")
    return jax.shard_map(local, mesh=mesh, in_specs=in_specs, out_specs=out_specs, check_vma=False)
```

```python
import functools

import jax
import jax.numpy as jnp
from jax import lax
from jax.experimental import pallas as pl
from jax.experimental.pallas import tpu as pltpu
from jax.sharding import PartitionSpec as P

MESH = pl.DeviceIdType.MESH
NY, NC = 4, 2
K = 64
KA = 80
KD = 72
PANEL = 8
sharpness = 10.0
epsilon = 1e-06

F32 = jnp.float32
BF16 = jnp.bfloat16
HIGH = lax.Precision.HIGHEST


def dot_nt(a, b, precision=None):
    return lax.dot_general(
        a, b, (((1,), (1,)), ((), ())), precision=precision, preferred_element_type=F32
    )


def dot_nn(a, b, precision=None):
    return jnp.dot(a, b, precision=precision, preferred_element_type=F32)


def normalize(src, dst, rows):
    width = src.shape[1]
    chunk = 64

    def body(c, carry):
        at = pl.ds(pl.multiple_of(c * chunk, chunk), chunk)
        values = src[at, :].astype(F32)
        square = jnp.sum(values * values, axis=1, keepdims=True) * (1.0 / width)
        scale = lax.rsqrt(square + epsilon) * (1.0 / width**0.5)
        dst[at, :] = (values * scale).astype(BF16)
        return carry

    lax.fori_loop(0, rows // chunk, body, 0, unroll=4)


def inverse_factor(matrix):
    wide = (8, 2 * K)
    lane = lax.broadcasted_iota(jnp.int32, wide, 1)
    row8 = lax.broadcasted_iota(jnp.int32, wide, 0)
    tall = K // 8

    def spread(values, k):
        return jnp.broadcast_to(values[:, k : k + 1], wide)

    matrix = jnp.concatenate([matrix, matrix], axis=1)
    blocks = [matrix[8 * m : 8 * m + 8, :] for m in range(tall)]
    marks = [lane == row8 + 8 * m for m in range(tall)]
    diagonals = [jnp.where(marks[m], blocks[m], 0.0) for m in range(tall)]
    along = sum(diagonals[1:], diagonals[0])
    along = jnp.broadcast_to(jnp.sum(along, axis=0, keepdims=True), wide)
    along = lax.rsqrt(jnp.where(lane < K, along, 1.0))
    work = []
    for m in range(tall):
        down = lax.rsqrt(jnp.broadcast_to(jnp.sum(diagonals[m], axis=1, keepdims=True), wide))
        right = jnp.where(lane - K == row8 + 8 * m, down, 0.0)
        work.append(jnp.where(lane < K, blocks[m] * down * along, right))
    done = []
    for m0 in range(tall):
        k = m0 * PANEL
        rows = [jnp.broadcast_to(work[m0][t : t + 1, :], wide) for t in range(PANEL)]
        a = {(t, u): spread(rows[t], k + u) for t in range(PANEL) for u in range(t, PANEL)}
        low, inv, pivot = {}, [None] * PANEL, [None] * PANEL
        for t in range(0, PANEL, 2):
            p, q = a[t, t], a[t, t + 1]
            det = p * a[t + 1, t + 1] - q * q
            inv[t] = 1.0 / p
            inv[t + 1] = p * (1.0 / det)
            pivot[t], pivot[t + 1] = p, det * inv[t]
            low[t + 1, t] = q * inv[t]
            for u in range(t + 2, PANEL):
                low[u, t] = a[t, u] * inv[t]
                a[t + 1, u] = a[t + 1, u] - low[t + 1, t] * a[t, u]
                low[u, t + 1] = a[t + 1, u] * inv[t + 1]
            for u in range(t + 2, PANEL):
                for v in range(u, PANEL):
                    a[u, v] = a[u, v] - low[u, t] * a[t, v] - low[u, t + 1] * a[t + 1, v]
        for t in range(1, PANEL):
            for u in range(t):
                rows[t] = rows[t] - low[t, u] * rows[u]
        scaled = [rows[t] * inv[t] for t in range(PANEL)]
        for m in range(m0 + 1, tall):
            column = [spread(work[m], k + t) for t in range(PANEL)]
            for t in range(1, PANEL):
                for u in range(t):
                    column[t] = column[t] - low[t, u] * column[u]
            for t in range(PANEL):
                work[m] = work[m] - column[t] * scaled[t]
        reduced, pivots = rows[0], pivot[0]
        for t in range(1, PANEL):
            reduced = jnp.where(row8 == t, rows[t], reduced)
            pivots = jnp.where(row8 == t, pivot[t], pivots)
        done.append(reduced * lax.rsqrt(pivots))
    return jnp.concatenate(done, axis=0)[:, K:]


def kernel(
    nz, ny, nc, nx, total_rows,
    emb, knn_in, prow_in, pcol_in, pcnt_in, start,
    out,
    knn, prow, pcol, pcnt, out_v, emb_v, unit, emb_h, unit_h, km, km_h, mcol, v0, v0_h, aff, part1, half1, part2, rs1, rs1_d, rs2,
    nar, nar_h, mask, mask_x, msum, yall, gpart, ga, gsum, gb, gsum2, gc, gfull,
    local_sem, out_sem, emb_s, emb_r, km_s, km_r, v0_s, v0_r, mask_s, mask_r,
    rs1_s, rs1_r, rsd_s, rsd_r, rs2_s, rs2_r, nar_s, nar_r, y_s, y_r,
    ga_s, ga_r, gb_s, gb_r, gc_s, gc_r, gd_s, gd_r, reach_sem,
):
    g = lax.axis_index("rows")
    x = lax.axis_index("cols")
    rows = nz * ny * nc
    core = g % nc
    y = (g // nc) % ny
    z = g // (nc * ny)
    block = emb_h.shape[1]
    here = emb_v.shape[0]
    blocks = here // block
    parts = nc * nx

    def at(dz=0, dy=0, dc=0, dx=0):
        row = (((z + dz) % nz) * ny + (y + dy) % ny) * nc + (core + dc) % nc
        return (row, (x + dx) % nx)

    sides = [((g + 1) % rows, x), ((g + rows - 1) % rows, x)]
    near = [(e // nx, e % nx) for e in range(1, parts)]
    xpeers = [at(dx=d) for d in range(1, nx)]
    npeers = [at(dc=dc, dx=dx) for dc, dx in near]
    ypeers = [at(dy=d) for d in range(1, ny)]
    zpeers = [at(dz=d) for d in range(1, nz)]

    barrier = pltpu.get_barrier_semaphore()
    zreach = [d for d in range(1, nz) if min(d, nz - d) <= 2]
    rounds = []
    while 2 * 2 ** len(rounds) < nz // 2:
        rounds.append(2 * 2 ** len(rounds))
    everyone = sides + npeers + ypeers + [at(dz=d) for d in zreach]
    for peer in everyone:
        pl.semaphore_signal(barrier, inc=1, device_id=peer, device_id_type=MESH)

    started = []

    def remote(src, dst, ssem, rsem, peer):
        return pltpu.make_async_remote_copy(
            src_ref=src, dst_ref=dst, send_sem=ssem, recv_sem=rsem,
            device_id=peer, device_id_type=MESH,
        )

    def send(src, dst, ssem, rsem, peer):
        copy = remote(src, dst, ssem, rsem, peer)
        copy.start()
        started.append(copy)
        return copy

    def reach_signal(n):
        for dz in (rounds[n], -rounds[n]):
            pl.semaphore_signal(
                reach_sem.at[n], inc=1, device_id=at(dz=nz + dz), device_id_type=MESH
            )

    own = pl.ds(pl.multiple_of(x * block, block), block)
    tables = [
        pltpu.make_async_copy(src, dst, local_sem.at[blocks + 1 + n])
        for n, (src, dst) in enumerate(
            ((knn_in, knn), (prow_in, prow), (pcol_in, pcol), (pcnt_in, pcnt))
        )
    ]
    for c in tables:
        c.start()
    for r in range(blocks):
        pltpu.make_async_copy(
            emb.at[pl.ds(r * block, block)], emb_v.at[pl.ds(r * block, block)], local_sem.at[r]
        ).start()
    load_v = pltpu.make_async_copy(start.at[:, own], v0, local_sem.at[blocks])
    load_v.start()

    pl.semaphore_wait(barrier, len(everyone))

    for h, peer in enumerate(sides):
        send(emb.at[own], emb_h.at[h], emb_s.at[h], emb_r.at[h], peer)

    for c in tables:
        c.wait()
    slots = prow.shape[-1]
    spot = (prow[0] - g * blocks) * (3 * blocks) + (pcol[0] - (g - 1) * blocks)
    live = lax.broadcasted_iota(jnp.int32, (1, slots), 1) < pcnt[...]
    spot = jnp.where(live, spot, -1)
    hit = lax.broadcasted_iota(jnp.int32, (mask.shape[0], slots), 0) == spot
    mask[...] = jnp.broadcast_to(
        jnp.sum(jnp.where(hit, 1.0, 0.0), axis=1, keepdims=True), mask.shape
    )
    means = knn[...].astype(F32).reshape(1, here)
    for r in range(blocks):
        km[r] = jnp.broadcast_to(means[:, r * block : (r + 1) * block], (8, block))
    for h, peer in enumerate(sides):
        send(km.at[x], km_h.at[h], km_s.at[h], km_r.at[h], peer)
    for h, peer in enumerate(sides):
        send(start.at[:, own], v0_h.at[h], v0_s.at[h], v0_r.at[h], peer)
    masks = [
        send(mask, mask_x.at[d], mask_s.at[d], mask_r.at[d], peer) for d, peer in enumerate(xpeers)
    ]
    if rounds:
        reach_signal(0)

    for r in range(blocks):
        where = pl.ds(r * block, block)
        pltpu.make_async_copy(emb.at[where], emb_v.at[where], local_sem.at[r]).wait()
        normalize(emb_v.at[where], unit.at[where], block)
    lane = lax.broadcasted_iota(jnp.int32, (block, block), 1)
    line = lax.broadcasted_iota(jnp.int32, (block, block), 0)
    eye = jnp.where(lane == line, 1.0, 0.0).astype(BF16)
    for r in range(blocks):
        wide = jnp.broadcast_to(km[r, 0:1, :], (128, block)).astype(BF16)
        mcol[pl.ds(r * block, block), :] = dot_nt(eye, wide)

    def affinity(slot, unit_col, mean_row, diagonal):
        for r in range(blocks):
            rows_at = pl.ds(r * block, block)
            scores = dot_nt(unit[rows_at, :], unit_col)
            side = jnp.concatenate([mcol[rows_at, :]] * (block // 128), axis=1)
            denom = 0.5 * (side + mean_row)
            weights = jnp.exp(sharpness * scores / denom)
            if diagonal:
                weights = jnp.where((lane == line) & (x == r), 0.0, weights)
            aff[slot, rows_at, :] = weights.astype(BF16)

    def product(slot, window, source, part, first):
        for r in range(blocks):
            live_pair = msum[pl.ds(r * 3 * blocks + window * blocks + x, 1), :][:, 0:1]
            piece = dot_nt(source, aff[slot, pl.ds(r * block, block), :]) * live_pair
            part[r, pl.ds(0, piece.shape[0]), :] = (
                piece if first else part[r, pl.ds(0, piece.shape[0]), :] + piece
            )

    tail = lax.broadcasted_iota(jnp.int32, (KA - K, block), 0)
    ones = jnp.where(tail == 0, 1.0, 0.0)

    def widened(values):
        return jnp.concatenate([values, ones], axis=0).astype(BF16)

    affinity(2, unit[own, :], km[x, 0:1, :], True)
    for c in masks:
        c.wait_recv()
    msum[...] = mask[...]
    for d in range(nx - 1):
        msum[...] += mask_x[d]
    load_v.wait()
    product(2, 1, widened(v0[...]), part1, True)

    for n in range(len(rounds)):
        pl.semaphore_wait(reach_sem.at[n], 2)
        if n + 1 < len(rounds):
            reach_signal(n + 1)

    def side(step, carry):
        h = (core + 1 + step) % 2
        remote(km.at[x], km_h.at[h], km_s.at[h], km_r.at[h], sides[0]).wait_recv()
        remote(emb.at[own], emb_h.at[h], emb_s.at[h], emb_r.at[h], sides[0]).wait_recv()
        normalize(emb_h.at[h], unit_h, block)
        affinity(h, unit_h[...], km_h[h, 0:1, :], False)
        remote(start.at[:, own], v0_h.at[h], v0_s.at[h], v0_r.at[h], sides[0]).wait_recv()
        product(h, 2 * h, widened(v0_h[h]), part1, False)
        return carry

    lax.fori_loop(0, 2, side, 0)

    for r in range(blocks):
        half1[r] = part1[r, pl.ds(0, K), :].astype(BF16)
    scatter = []
    for d, peer in zip(range(1, nx), xpeers):
        p, e = (x + d) % nx, d - 1
        scatter.append(send(half1.at[p], rs1.at[e], rs1_s.at[e], rs1_r.at[e], peer))
        scatter.append(
            send(part1.at[p, pl.ds(K, KD - K)], rs1_d.at[e], rsd_s.at[e], rsd_r.at[e], peer)
        )
    for c in scatter:
        c.wait_recv()
    total = part1[x, pl.ds(0, K), :]
    degree = part1[x, pl.ds(K, KD - K), :]
    for d in range(nx - 1):
        total = total + rs1[d].astype(F32)
        degree = degree + rs1_d[d]
    degree = degree[0:1, :]
    smoothed1 = total / degree
    nar[...] = smoothed1.astype(BF16)

    height = K // 2 // parts
    me = core * nx + x

    def gram_a(q, smoothed):
        gram = dot_nt(smoothed, smoothed, HIGH) * (1.0 / total_rows)
        gram = jnp.concatenate([gram[: K // 2], gram[K // 2 :]], axis=1)
        for p in range(parts):
            gpart[q, p] = gram[p * height : (p + 1) * height, :]
        return [
            send(
                gpart.at[q, ((core + dc) % nc) * nx + (x + dx) % nx],
                ga.at[q, e], ga_s.at[q, e], ga_r.at[q, e], peer,
            )
            for e, ((dc, dx), peer) in enumerate(zip(near, npeers))
        ]

    def gram_b(q, copies):
        for c in copies:
            c.wait_recv()
        total = gpart[q, me]
        for e in range(parts - 1):
            total = total + ga[q, e]
        gsum[q] = total
        return [
            send(gsum.at[q], gb.at[q, d], gb_s.at[q, d], gb_r.at[q, d], peer)
            for d, peer in enumerate(ypeers)
        ]

    def gram_c(q, copies):
        for c in copies:
            c.wait_recv()
        total = gsum[q]
        for d in range(ny - 1):
            total = total + gb[q, d]
        gsum2[q] = total
        return [
            send(gsum2.at[q], gc.at[q, d], gc_s.at[q, d], gc_r.at[q, d], peer)
            for d, peer in enumerate(zpeers)
        ]

    def gram_d(q, copies):
        for c in copies:
            c.wait_recv()
        total = gsum2[q]
        for d in range(nz - 1):
            total = total + gc[q, d]
        gfull[q, 0] = total
        return [
            send(gfull.at[q, 0], gfull.at[q, e + 1], gd_s.at[q, e], gd_r.at[q, e], peer)
            for e, peer in enumerate(npeers)
        ]

    def gram_whole(q, copies):
        for c in copies:
            c.wait_recv()
        pieces = [
            gfull[q, ((core + nc - p // nx) % nc) * nx + (x + nx - p % nx) % nx]
            for p in range(parts)
        ]
        packed = jnp.concatenate(pieces, axis=0)
        return jnp.concatenate([packed[:, :K], packed[:, K:]], axis=0)

    narrow = [send(nar, nar_h.at[h], nar_s.at[h], nar_r.at[h], peer) for h, peer in enumerate(sides)]
    sum1 = gram_a(0, smoothed1)
    product(2, 1, nar[...], part2, True)
    for c in narrow:
        c.wait_recv()
    for h in range(2):
        product(h, 2 * h, nar_h[h], part2, False)
    scatter = [
        send(part2.at[(x + d) % nx], rs2.at[d - 1], rs2_s.at[d - 1], rs2_r.at[d - 1], peer)
        for d, peer in zip(range(1, nx), xpeers)
    ]
    sum1 = gram_c(0, gram_b(0, sum1))
    for c in scatter:
        c.wait_recv()
    total = part2[x]
    for d in range(nx - 1):
        total = total + rs2[d]
    smoothed2 = total / degree
    yall[0] = smoothed2
    sum2 = gram_b(1, gram_a(1, smoothed2))
    gather = [
        send(yall.at[0], yall.at[d], y_s.at[d - 1], y_r.at[d - 1], peer)
        for d, peer in zip(range(1, nx), xpeers)
    ]
    sum2 = gram_c(1, sum2)
    first = inverse_factor(gram_whole(0, gram_d(0, sum1)))
    for c in gather:
        c.wait_recv()
    once = [dot_nn(first, yall[(x + nx - p) % nx], HIGH) for p in range(nx)]
    for p in range(nx):
        out_v[p] = once[p]
    gram = gram_whole(1, gram_d(1, sum2))

    second = inverse_factor(dot_nt(dot_nn(first, gram, HIGH), first, HIGH))
    stores = []
    for p in range(nx):
        out_v[p] = dot_nn(second, out_v[p], HIGH)
        stores.append(
            pltpu.make_async_copy(out_v.at[p], out.at[:, pl.ds(p * block, block)], out_sem.at[p])
        )
        stores[p].start()
    for c in started:
        c.wait_send()
    for c in stores:
        c.wait()


def solution(mesh):
    nx = mesh.shape["cols"]
    groups = mesh.shape["rows"]
    nz = groups // (NY * NC)
    parts = NC * nx

    def local(embeddings, knn_mean, pair_rows, pair_cols, pair_count, start_block):
        here, width = embeddings.shape
        block = here // nx
        height = K // 2 // parts
        dma = pltpu.SemaphoreType.DMA
        hbm = pl.BlockSpec(memory_space=pl.ANY)
        return pl.pallas_call(
            functools.partial(kernel, nz, NY, NC, nx, here * groups),
            out_shape=jax.ShapeDtypeStruct((K, here), F32),
            in_specs=[hbm] * 6,
            out_specs=hbm,
            scratch_shapes=[
                pltpu.VMEM(knn_mean.shape, BF16),
                pltpu.VMEM(pair_rows.shape, jnp.int32),
                pltpu.VMEM(pair_cols.shape, jnp.int32),
                pltpu.VMEM(pair_count.shape, jnp.int32),
                pltpu.VMEM((nx, K, block), F32),
                pltpu.VMEM((here, width), BF16),
                pltpu.VMEM((here, width), BF16),
                pltpu.VMEM((2, block, width), BF16),
                pltpu.VMEM((block, width), BF16),
                pltpu.VMEM((nx, 8, block), F32),
                pltpu.VMEM((2, 8, block), F32),
                pltpu.VMEM((here, 128), F32),
                pltpu.VMEM((K, block), F32),
                pltpu.VMEM((2, K, block), F32),
                pltpu.VMEM((3, here, block), BF16),
                pltpu.VMEM((nx, KA, block), F32),
                pltpu.VMEM((nx, K, block), BF16),
                pltpu.VMEM((nx, K, block), F32),
                pltpu.VMEM((nx - 1, K, block), BF16),
                pltpu.VMEM((nx - 1, KD - K, block), F32),
                pltpu.VMEM((nx - 1, K, block), F32),
                pltpu.VMEM((K, block), BF16),
                pltpu.VMEM((2, K, block), BF16),
                pltpu.VMEM((3 * nx * nx, 128), F32),
                pltpu.VMEM((nx - 1, 3 * nx * nx, 128), F32),
                pltpu.VMEM((3 * nx * nx, 128), F32),
                pltpu.VMEM((nx, K, block), F32),
                pltpu.VMEM((2, parts, height, 2 * K), F32),
                pltpu.VMEM((2, parts - 1, height, 2 * K), F32),
                pltpu.VMEM((2, height, 2 * K), F32),
                pltpu.VMEM((2, NY - 1, height, 2 * K), F32),
                pltpu.VMEM((2, height, 2 * K), F32),
                pltpu.VMEM((2, nz - 1, height, 2 * K), F32),
                pltpu.VMEM((2, parts, height, 2 * K), F32),
                dma((nx + 5,)), dma((nx,)),
                dma((2,)), dma((2,)), dma((2,)), dma((2,)), dma((2,)), dma((2,)),
                dma((nx - 1,)), dma((nx - 1,)),
                dma((nx - 1,)), dma((nx - 1,)), dma((nx - 1,)), dma((nx - 1,)),
                dma((nx - 1,)), dma((nx - 1,)),
                dma((2,)), dma((2,)),
                dma((nx - 1,)), dma((nx - 1,)),
                dma((2, parts - 1)), dma((2, parts - 1)),
                dma((2, NY - 1)), dma((2, NY - 1)),
                dma((2, nz - 1)), dma((2, nz - 1)),
                dma((2, parts - 1)), dma((2, parts - 1)),
                pltpu.SemaphoreType.REGULAR((4,)),
            ],
            compiler_params=pltpu.CompilerParams(collective_id=0, has_side_effects=True),
        )(embeddings, knn_mean, pair_rows, pair_cols, pair_count, start_block)

    in_specs = (
        P("rows", None),
        P("rows"),
        P("rows", "cols", None),
        P("rows", "cols", None),
        P("rows", "cols"),
        P(None, "rows"),
    )
    out_specs = P(None, "rows")
    return jax.shard_map(local, mesh=mesh, in_specs=in_specs, out_specs=out_specs, check_vma=False)
```

```python
import functools

import jax
import jax.numpy as jnp
from jax import lax
from jax.experimental import pallas as pl
from jax.experimental.pallas import tpu as pltpu
from jax.sharding import PartitionSpec as P

MESH = pl.DeviceIdType.MESH
NY, NC = 4, 2
K = 64
KA = 80
KD = 72
PANEL = 8
sharpness = 10.0
epsilon = 1e-06

F32 = jnp.float32
BF16 = jnp.bfloat16
HIGH = lax.Precision.HIGHEST


def dot_nt(a, b, precision=None):
    return lax.dot_general(
        a, b, (((1,), (1,)), ((), ())), precision=precision, preferred_element_type=F32
    )


def dot_nn(a, b, precision=None):
    return jnp.dot(a, b, precision=precision, preferred_element_type=F32)


def normalize(src, dst, rows):
    width = src.shape[1]
    chunk = 64

    def body(c, carry):
        at = pl.ds(pl.multiple_of(c * chunk, chunk), chunk)
        values = src[at, :].astype(F32)
        square = jnp.sum(values * values, axis=1, keepdims=True) * (1.0 / width)
        scale = lax.rsqrt(square + epsilon) * (1.0 / width**0.5)
        dst[at, :] = (values * scale).astype(BF16)
        return carry

    lax.fori_loop(0, rows // chunk, body, 0, unroll=4)


def inverse_factor(matrix):
    wide = (8, 2 * K)
    lane = lax.broadcasted_iota(jnp.int32, wide, 1)
    row8 = lax.broadcasted_iota(jnp.int32, wide, 0)
    tall = K // 8

    def spread(values, k):
        return jnp.broadcast_to(values[:, k : k + 1], wide)

    matrix = jnp.concatenate([matrix, matrix], axis=1)
    blocks = [matrix[8 * m : 8 * m + 8, :] for m in range(tall)]
    marks = [lane == row8 + 8 * m for m in range(tall)]
    diagonals = [jnp.where(marks[m], blocks[m], 0.0) for m in range(tall)]
    along = sum(diagonals[1:], diagonals[0])
    along = jnp.broadcast_to(jnp.sum(along, axis=0, keepdims=True), wide)
    along = lax.rsqrt(jnp.where(lane < K, along, 1.0))
    work = []
    for m in range(tall):
        down = lax.rsqrt(jnp.broadcast_to(jnp.sum(diagonals[m], axis=1, keepdims=True), wide))
        right = jnp.where(lane - K == row8 + 8 * m, down, 0.0)
        work.append(jnp.where(lane < K, blocks[m] * down * along, right))
    done = []
    for m0 in range(tall):
        k = m0 * PANEL
        rows = [jnp.broadcast_to(work[m0][t : t + 1, :], wide) for t in range(PANEL)]
        a = {(t, u): spread(rows[t], k + u) for t in range(PANEL) for u in range(t, PANEL)}
        low, inv, pivot = {}, [None] * PANEL, [None] * PANEL
        for t in range(0, PANEL, 2):
            p, q = a[t, t], a[t, t + 1]
            det = p * a[t + 1, t + 1] - q * q
            inv[t] = 1.0 / p
            inv[t + 1] = p * (1.0 / det)
            pivot[t], pivot[t + 1] = p, det * inv[t]
            low[t + 1, t] = q * inv[t]
            for u in range(t + 2, PANEL):
                low[u, t] = a[t, u] * inv[t]
                a[t + 1, u] = a[t + 1, u] - low[t + 1, t] * a[t, u]
                low[u, t + 1] = a[t + 1, u] * inv[t + 1]
            for u in range(t + 2, PANEL):
                for v in range(u, PANEL):
                    a[u, v] = a[u, v] - low[u, t] * a[t, v] - low[u, t + 1] * a[t + 1, v]
        for t in range(1, PANEL):
            for u in range(t):
                rows[t] = rows[t] - low[t, u] * rows[u]
        scaled = [rows[t] * inv[t] for t in range(PANEL)]
        for m in range(m0 + 1, tall):
            column = [spread(work[m], k + t) for t in range(PANEL)]
            for t in range(1, PANEL):
                for u in range(t):
                    column[t] = column[t] - low[t, u] * column[u]
            for t in range(PANEL):
                work[m] = work[m] - column[t] * scaled[t]
        reduced, pivots = rows[0], pivot[0]
        for t in range(1, PANEL):
            reduced = jnp.where(row8 == t, rows[t], reduced)
            pivots = jnp.where(row8 == t, pivot[t], pivots)
        done.append(reduced * lax.rsqrt(pivots))
    return jnp.concatenate(done, axis=0)[:, K:]


def kernel(
    nz, ny, nc, nx, total_rows,
    emb, knn_in, prow_in, pcol_in, pcnt_in, start,
    out,
    knn, prow, pcol, pcnt, out_v, emb_v, unit, emb_h, unit_h, km, km_h, mcol, v0, v0_h, aff, part1, half1, part2, rs1, rs1_d, rs2,
    nar, nar_h, mask, mask_x, msum, yall, gpart, ga, gsum, gb, gsum2, gc, gfull,
    local_sem, out_sem, emb_s, emb_r, km_s, km_r, v0_s, v0_r, mask_s, mask_r,
    rs1_s, rs1_r, rsd_s, rsd_r, rs2_s, rs2_r, nar_s, nar_r, y_s, y_r,
    ga_s, ga_r, gb_s, gb_r, gc_s, gc_r, gd_s, gd_r, reach_sem,
):
    g = lax.axis_index("rows")
    x = lax.axis_index("cols")
    rows = nz * ny * nc
    core = g % nc
    y = (g // nc) % ny
    z = g // (nc * ny)
    block = emb_h.shape[1]
    here = emb_v.shape[0]
    blocks = here // block
    parts = nc * nx

    def at(dz=0, dy=0, dc=0, dx=0):
        row = (((z + dz) % nz) * ny + (y + dy) % ny) * nc + (core + dc) % nc
        return (row, (x + dx) % nx)

    sides = [((g + rows + 2 * core - 1) % rows, x), ((g + rows + 1 - 2 * core) % rows, x)]
    lands = [1 - core, core]
    comes = [core, 1 - core]
    near = [(e // nx, e % nx) for e in range(1, parts)]
    xpeers = [at(dx=d) for d in range(1, nx)]
    npeers = [at(dc=dc, dx=dx) for dc, dx in near]
    ypeers = [at(dy=d) for d in range(1, ny)]
    zpeers = [at(dz=d) for d in range(1, nz)]

    barrier = pltpu.get_barrier_semaphore()
    zreach = [d for d in range(1, nz) if min(d, nz - d) <= 2]
    rounds = []
    while 2 * 2 ** len(rounds) < nz // 2:
        rounds.append(2 * 2 ** len(rounds))
    everyone = sides + npeers + ypeers + [at(dz=d) for d in zreach]
    for peer in everyone:
        pl.semaphore_signal(barrier, inc=1, device_id=peer, device_id_type=MESH)

    started = []

    def remote(src, dst, ssem, rsem, peer):
        return pltpu.make_async_remote_copy(
            src_ref=src, dst_ref=dst, send_sem=ssem, recv_sem=rsem,
            device_id=peer, device_id_type=MESH,
        )

    def send(src, dst, ssem, rsem, peer):
        copy = remote(src, dst, ssem, rsem, peer)
        copy.start()
        started.append(copy)
        return copy

    def reach_signal(n):
        for dz in (rounds[n], -rounds[n]):
            pl.semaphore_signal(
                reach_sem.at[n], inc=1, device_id=at(dz=nz + dz), device_id_type=MESH
            )

    own = pl.ds(pl.multiple_of(x * block, block), block)
    tables = [
        pltpu.make_async_copy(src, dst, local_sem.at[blocks + 1 + n])
        for n, (src, dst) in enumerate(
            ((knn_in, knn), (prow_in, prow), (pcol_in, pcol), (pcnt_in, pcnt))
        )
    ]
    for c in tables:
        c.start()
    for r in range(blocks):
        pltpu.make_async_copy(
            emb.at[pl.ds(r * block, block)], emb_v.at[pl.ds(r * block, block)], local_sem.at[r]
        ).start()
    load_v = pltpu.make_async_copy(start.at[:, own], v0, local_sem.at[blocks])
    load_v.start()

    pl.semaphore_wait(barrier, len(everyone))

    for h, peer in zip(lands, sides):
        send(emb.at[own], emb_h.at[h], emb_s.at[h], emb_r.at[h], peer)

    for c in tables:
        c.wait()
    slots = prow.shape[-1]
    spot = (prow[0] - g * blocks) * (3 * blocks) + (pcol[0] - (g - 1) * blocks)
    live = lax.broadcasted_iota(jnp.int32, (1, slots), 1) < pcnt[...]
    spot = jnp.where(live, spot, -1)
    hit = lax.broadcasted_iota(jnp.int32, (mask.shape[0], slots), 0) == spot
    mask[...] = jnp.broadcast_to(
        jnp.sum(jnp.where(hit, 1.0, 0.0), axis=1, keepdims=True), mask.shape
    )
    means = knn[...].astype(F32).reshape(1, here)
    for r in range(blocks):
        km[r] = jnp.broadcast_to(means[:, r * block : (r + 1) * block], (8, block))
    for h, peer in zip(lands, sides):
        send(km.at[x], km_h.at[h], km_s.at[h], km_r.at[h], peer)
    for h, peer in zip(lands, sides):
        send(start.at[:, own], v0_h.at[h], v0_s.at[h], v0_r.at[h], peer)
    masks = [
        send(mask, mask_x.at[d], mask_s.at[d], mask_r.at[d], peer) for d, peer in enumerate(xpeers)
    ]
    if rounds:
        reach_signal(0)

    for r in range(blocks):
        where = pl.ds(r * block, block)
        pltpu.make_async_copy(emb.at[where], emb_v.at[where], local_sem.at[r]).wait()
        normalize(emb_v.at[where], unit.at[where], block)
    lane = lax.broadcasted_iota(jnp.int32, (block, block), 1)
    line = lax.broadcasted_iota(jnp.int32, (block, block), 0)
    eye = jnp.where(lane == line, 1.0, 0.0).astype(BF16)
    for r in range(blocks):
        wide = jnp.broadcast_to(km[r, 0:1, :], (128, block)).astype(BF16)
        mcol[pl.ds(r * block, block), :] = dot_nt(eye, wide)

    def affinity(slot, unit_col, mean_row, diagonal):
        for r in range(blocks):
            rows_at = pl.ds(r * block, block)
            scores = dot_nt(unit[rows_at, :], unit_col)
            side = jnp.concatenate([mcol[rows_at, :]] * (block // 128), axis=1)
            denom = 0.5 * (side + mean_row)
            weights = jnp.exp(sharpness * scores / denom)
            if diagonal:
                weights = jnp.where((lane == line) & (x == r), 0.0, weights)
            aff[slot, rows_at, :] = weights.astype(BF16)

    order = sorted(range(nx), key=lambda d: -min(d, nx - d))

    def product(slot, window, source, part, first, finish=None):
        height = source.shape[0]
        for d in order:
            p = (x + d) % nx
            live_pair = msum[pl.ds(p * 3 * blocks + window * blocks + x, 1), :][:, 0:1]
            rows_at = pl.ds(pl.multiple_of(p * block, block), block)
            piece = dot_nt(source, aff[slot, rows_at, :]) * live_pair
            if not first:
                piece = part[p, pl.ds(0, height), :] + piece
            part[p, pl.ds(0, height), :] = piece
            if finish is not None and d > 0:
                finish(d, p, piece)

    tail = lax.broadcasted_iota(jnp.int32, (KA - K, block), 0)
    ones = jnp.where(tail == 0, 1.0, 0.0)

    def widened(values):
        return jnp.concatenate([values, ones], axis=0).astype(BF16)

    affinity(2, unit[own, :], km[x, 0:1, :], True)
    for c in masks:
        c.wait_recv()
    msum[...] = mask[...]
    for d in range(nx - 1):
        msum[...] += mask_x[d]
    load_v.wait()
    product(2, 1, widened(v0[...]), part1, True)

    for n in range(len(rounds)):
        pl.semaphore_wait(reach_sem.at[n], 2)
        if n + 1 < len(rounds):
            reach_signal(n + 1)

    scatter = []

    def scatter1(d, p, values):
        e, peer = d - 1, xpeers[d - 1]
        half1[p] = values[:K].astype(BF16)
        scatter.append(send(half1.at[p], rs1.at[e], rs1_s.at[e], rs1_r.at[e], peer))
        scatter.append(
            send(part1.at[p, pl.ds(K, KD - K)], rs1_d.at[e], rsd_s.at[e], rsd_r.at[e], peer)
        )

    for n in (1, 0):
        h = comes[n]
        remote(km.at[x], km_h.at[h], km_s.at[h], km_r.at[h], sides[0]).wait_recv()
        remote(emb.at[own], emb_h.at[h], emb_s.at[h], emb_r.at[h], sides[0]).wait_recv()
        normalize(emb_h.at[h], unit_h, block)
        affinity(h, unit_h[...], km_h[h, 0:1, :], False)
        remote(start.at[:, own], v0_h.at[h], v0_s.at[h], v0_r.at[h], sides[0]).wait_recv()
        product(h, 2 * h, widened(v0_h[h]), part1, False, None if n else scatter1)

    for c in scatter:
        c.wait_recv()
    total = part1[x, pl.ds(0, K), :]
    degree = part1[x, pl.ds(K, KD - K), :]
    for d in range(nx - 1):
        total = total + rs1[d].astype(F32)
        degree = degree + rs1_d[d]
    degree = degree[0:1, :]
    smoothed1 = total / degree
    nar[...] = smoothed1.astype(BF16)

    height = K // 2 // parts
    me = core * nx + x

    def gram_a(q, smoothed):
        gram = dot_nt(smoothed, smoothed, HIGH) * (1.0 / total_rows)
        gram = jnp.concatenate([gram[: K // 2], gram[K // 2 :]], axis=1)
        for p in range(parts):
            gpart[q, p] = gram[p * height : (p + 1) * height, :]
        return [
            send(
                gpart.at[q, ((core + dc) % nc) * nx + (x + dx) % nx],
                ga.at[q, e], ga_s.at[q, e], ga_r.at[q, e], peer,
            )
            for e, ((dc, dx), peer) in enumerate(zip(near, npeers))
        ]

    def gram_b(q, copies):
        for c in copies:
            c.wait_recv()
        total = gpart[q, me]
        for e in range(parts - 1):
            total = total + ga[q, e]
        gsum[q] = total
        return [
            send(gsum.at[q], gb.at[q, d], gb_s.at[q, d], gb_r.at[q, d], peer)
            for d, peer in enumerate(ypeers)
        ]

    def gram_c(q, copies):
        for c in copies:
            c.wait_recv()
        total = gsum[q]
        for d in range(ny - 1):
            total = total + gb[q, d]
        gsum2[q] = total
        return [
            send(gsum2.at[q], gc.at[q, d], gc_s.at[q, d], gc_r.at[q, d], peer)
            for d, peer in sorted(enumerate(zpeers), key=lambda item: -min(item[0] + 1, nz - item[0] - 1))
        ]

    def gram_d(q, copies):
        for c in copies:
            c.wait_recv()
        total = gsum2[q]
        for d in range(nz - 1):
            total = total + gc[q, d]
        gfull[q, 0] = total
        return [
            send(gfull.at[q, 0], gfull.at[q, e + 1], gd_s.at[q, e], gd_r.at[q, e], peer)
            for e, peer in enumerate(npeers)
        ]

    def gram_whole(q, copies):
        for c in copies:
            c.wait_recv()
        pieces = [
            gfull[q, ((core + nc - p // nx) % nc) * nx + (x + nx - p % nx) % nx]
            for p in range(parts)
        ]
        packed = jnp.concatenate(pieces, axis=0)
        return jnp.concatenate([packed[:, :K], packed[:, K:]], axis=0)

    for h, peer in zip(lands, sides):
        send(nar, nar_h.at[h], nar_s.at[h], nar_r.at[h], peer)
    sum1 = gram_a(0, smoothed1)
    product(2, 1, nar[...], part2, True)
    scatter = []

    def scatter2(d, p, values):
        e = d - 1
        scatter.append(send(part2.at[p], rs2.at[e], rs2_s.at[e], rs2_r.at[e], xpeers[e]))

    for n in (1, 0):
        h = comes[n]
        remote(nar, nar_h.at[h], nar_s.at[h], nar_r.at[h], sides[0]).wait_recv()
        product(h, 2 * h, nar_h[h], part2, False, None if n else scatter2)
    sum1 = gram_c(0, gram_b(0, sum1))
    for c in scatter:
        c.wait_recv()
    total = part2[x]
    for d in range(nx - 1):
        total = total + rs2[d]
    smoothed2 = total / degree
    yall[0] = smoothed2
    sum2 = gram_b(1, gram_a(1, smoothed2))
    gather = [
        send(yall.at[0], yall.at[d], y_s.at[d - 1], y_r.at[d - 1], peer)
        for d, peer in zip(range(1, nx), xpeers)
    ]
    sum2 = gram_c(1, sum2)
    first = inverse_factor(gram_whole(0, gram_d(0, sum1)))
    for c in gather:
        c.wait_recv()
    once = [dot_nn(first, yall[(x + nx - p) % nx], HIGH) for p in range(nx)]
    for p in range(nx):
        out_v[p] = once[p]
    gram = gram_whole(1, gram_d(1, sum2))

    second = inverse_factor(dot_nt(dot_nn(first, gram, HIGH), first, HIGH))
    stores = []
    for p in range(nx):
        out_v[p] = dot_nn(second, out_v[p], HIGH)
        stores.append(
            pltpu.make_async_copy(out_v.at[p], out.at[:, pl.ds(p * block, block)], out_sem.at[p])
        )
        stores[p].start()
    for c in started:
        c.wait_send()
    for c in stores:
        c.wait()


def solution(mesh):
    nx = mesh.shape["cols"]
    groups = mesh.shape["rows"]
    nz = groups // (NY * NC)
    parts = NC * nx

    def local(embeddings, knn_mean, pair_rows, pair_cols, pair_count, start_block):
        here, width = embeddings.shape
        block = here // nx
        height = K // 2 // parts
        dma = pltpu.SemaphoreType.DMA
        hbm = pl.BlockSpec(memory_space=pl.ANY)
        return pl.pallas_call(
            functools.partial(kernel, nz, NY, NC, nx, here * groups),
            out_shape=jax.ShapeDtypeStruct((K, here), F32),
            in_specs=[hbm] * 6,
            out_specs=hbm,
            scratch_shapes=[
                pltpu.VMEM(knn_mean.shape, BF16),
                pltpu.VMEM(pair_rows.shape, jnp.int32),
                pltpu.VMEM(pair_cols.shape, jnp.int32),
                pltpu.VMEM(pair_count.shape, jnp.int32),
                pltpu.VMEM((nx, K, block), F32),
                pltpu.VMEM((here, width), BF16),
                pltpu.VMEM((here, width), BF16),
                pltpu.VMEM((2, block, width), BF16),
                pltpu.VMEM((block, width), BF16),
                pltpu.VMEM((nx, 8, block), F32),
                pltpu.VMEM((2, 8, block), F32),
                pltpu.VMEM((here, 128), F32),
                pltpu.VMEM((K, block), F32),
                pltpu.VMEM((2, K, block), F32),
                pltpu.VMEM((3, here, block), BF16),
                pltpu.VMEM((nx, KA, block), F32),
                pltpu.VMEM((nx, K, block), BF16),
                pltpu.VMEM((nx, K, block), F32),
                pltpu.VMEM((nx - 1, K, block), BF16),
                pltpu.VMEM((nx - 1, KD - K, block), F32),
                pltpu.VMEM((nx - 1, K, block), F32),
                pltpu.VMEM((K, block), BF16),
                pltpu.VMEM((2, K, block), BF16),
                pltpu.VMEM((3 * nx * nx, 128), F32),
                pltpu.VMEM((nx - 1, 3 * nx * nx, 128), F32),
                pltpu.VMEM((3 * nx * nx, 128), F32),
                pltpu.VMEM((nx, K, block), F32),
                pltpu.VMEM((2, parts, height, 2 * K), F32),
                pltpu.VMEM((2, parts - 1, height, 2 * K), F32),
                pltpu.VMEM((2, height, 2 * K), F32),
                pltpu.VMEM((2, NY - 1, height, 2 * K), F32),
                pltpu.VMEM((2, height, 2 * K), F32),
                pltpu.VMEM((2, nz - 1, height, 2 * K), F32),
                pltpu.VMEM((2, parts, height, 2 * K), F32),
                dma((nx + 5,)), dma((nx,)),
                dma((2,)), dma((2,)), dma((2,)), dma((2,)), dma((2,)), dma((2,)),
                dma((nx - 1,)), dma((nx - 1,)),
                dma((nx - 1,)), dma((nx - 1,)), dma((nx - 1,)), dma((nx - 1,)),
                dma((nx - 1,)), dma((nx - 1,)),
                dma((2,)), dma((2,)),
                dma((nx - 1,)), dma((nx - 1,)),
                dma((2, parts - 1)), dma((2, parts - 1)),
                dma((2, NY - 1)), dma((2, NY - 1)),
                dma((2, nz - 1)), dma((2, nz - 1)),
                dma((2, parts - 1)), dma((2, parts - 1)),
                pltpu.SemaphoreType.REGULAR((4,)),
            ],
            compiler_params=pltpu.CompilerParams(collective_id=0, has_side_effects=True),
        )(embeddings, knn_mean, pair_rows, pair_cols, pair_count, start_block)

    in_specs = (
        P("rows", None),
        P("rows"),
        P("rows", "cols", None),
        P("rows", "cols", None),
        P("rows", "cols"),
        P(None, "rows"),
    )
    out_specs = P(None, "rows")
    return jax.shard_map(local, mesh=mesh, in_specs=in_specs, out_specs=out_specs, check_vma=False)
```
